256 devices in a mesh: col: 64 (over z, x, core), rhs: 4 (over y).
Axes of the slice: x: 4, y: 4, z: 8, core: 2. Of those that a mesh axis runs over, the one named last changes fastest.
Arguments:
- rhs_block: bfloat16 [16384, 4096], P('col', 'rhs'), may hold values from -6 to 6
- solution: bfloat16 [196608, 4096], P('col', 'rhs'), may hold values from -6 to 6
- factor: bfloat16 [64, 6, 256, 3072], P('col', None, 'rhs'), may hold values from -0.109375 to 0.109375
- tile_list: int32 [64, 6], P('col'), may hold values 0 or 1
- diag_inverse: bfloat16 [64, 256, 256], P('col'), may hold values from -0.375 to 0.375
Outputs:
- solved_rows: bfloat16 [16384, 4096], P('col', 'rhs')
The draws below stay inside these ranges and needn't reach their ends.
All inputs are finite; a program needn't handle non-finite values. No bound on the sum of `tile_list` on one device may be relied on, other than what follows from the above.
Results may differ from the reference program's by a relative error of at most 0.0049.
Values may be sent and summed in bfloat16 or wider, within the bound.
A program may use at most 64 MiB of HBM per device.

```python
import jax
import jax.numpy as jnp
from jax import lax

BS = 256
XB = 1536
OWN_BLOCKS = 2
NRHS = 4096
HOPS = 6
ROWS = 16384
SOL_ROWS = 196608
N_COL = 64


def touch_ends(values, stream_key, least, high):
    longest = values.shape.index(max(values.shape))
    spots = []
    for shift in (0, 1):
        where = [jax.random.randint(jax.random.fold_in(stream_key, axis), (), 0, length) for axis, length in enumerate(values.shape)]
        where[longest] = (where[longest] + shift) % values.shape[longest]
        spots.append(tuple(where))
    return values.at[spots[0]].set(least).at[spots[1]].set(high)


def block_levels(stream_key, shape, cuts, least, high):
    factor_of = 1.0
    for position, blocks in cuts:
        heights = jax.random.uniform(jax.random.fold_in(jax.random.fold_in(stream_key, 6), position), (blocks,), jnp.float32, least / len(cuts), high / len(cuts))
        factor_of = factor_of * jnp.repeat(jnp.exp(heights), shape[position] // blocks).reshape((-1,) + (1,) * (len(shape) - 1 - position))
    return factor_of


def gaussian(key, shape, spread, reach, cuts=(), kind=jnp.bfloat16):
    factor_of = block_levels(key, shape, cuts, -0.22, 0.18) if cuts else 1.0
    result = jax.random.normal(key, shape, jnp.float32) * spread * factor_of
    return jnp.minimum(jnp.maximum(result, -reach), reach).astype(kind)


def setup_inputs(seed: int = 0) -> dict:
    key_list = jax.random.split(jax.random.key(seed), 6)
    rhs_block = gaussian(key_list[0], (ROWS, NRHS), 1.0, 6.0, ((0, 64), (1, 4)))
    solution = gaussian(key_list[1], (SOL_ROWS, NRHS), 1.0, 6.0, ((0, 64), (1, 4)))
    factor = gaussian(key_list[2], (N_COL, HOPS, BS, OWN_BLOCKS * XB), (OWN_BLOCKS * XB) ** -0.5, 0.109375, ((0, 64), (2, 4)))
    tile_list = touch_ends((jax.random.randint(key_list[3], (N_COL, HOPS), 0, 4) < 3).astype(jnp.int32), jax.random.fold_in(key_list[3], 1), 0, 1)
    diag_inverse = gaussian(key_list[4], (N_COL, BS, BS), BS ** -0.5, 0.375, ((0, 64),))
    return {"rhs_block": rhs_block, "solution": solution, "factor": factor, "tile_list": tile_list, "diag_inverse": diag_inverse}


def reference(rhs_block, solution, factor, tile_list, diag_inverse):
    owners = jnp.arange(N_COL, dtype=jnp.int32)
    weights = tile_list.astype(jnp.float32)
    solved = solution.reshape(N_COL, OWN_BLOCKS * XB, NRHS)
    rhs_rows = rhs_block.reshape(N_COL, BS, NRHS)

    def one_row(exit_row):
        total = jnp.zeros((BS, NRHS), jnp.float32)
        for offset in range(HOPS):
            source = ((exit_row - offset - 1 + N_COL) % N_COL).astype(jnp.int32)
            product = jnp.dot(factor[source, offset], solved[source], preferred_element_type=jnp.float32)
            total = total + product * weights[source, offset]
        remaining = (rhs_rows[exit_row].astype(jnp.float32) - total).astype(jnp.bfloat16)
        return jnp.dot(diag_inverse[exit_row], remaining, preferred_element_type=jnp.float32).astype(jnp.bfloat16)

    blocks = lax.map(one_row, owners)
    return blocks.reshape(N_COL * BS, NRHS)
```

```python
import functools

import jax
import jax.numpy as jnp
from jax import lax
from jax.experimental import pallas as pl
from jax.experimental.pallas import tpu as pltpu
from jax.sharding import PartitionSpec as P

MESH = pl.DeviceIdType.MESH


def kernel(n_col, n_rhs, order, tiles_ref, rhs_hbm, sol_hbm, fac_hbm, dia_hbm, out_ref,
           sol, fac, rhs, dia, acc, rem, part, got,
           load_sem, y_send, y_recv, x_send, x_recv):
    hops, quarter = fac_hbm.shape[1], fac_hbm.shape[2]
    rows, cols = rhs_hbm.shape
    half = quarter // 2
    wide = min(256, cols)
    col, row = lax.axis_index("col"), lax.axis_index("rhs")
    up, down = lax.rem(row + 1, n_rhs), lax.rem(row + n_rhs - 1, n_rhs)

    loads = [
        pltpu.make_async_copy(fac_hbm.at[0], fac.at[:, pl.ds(0, quarter), :], load_sem.at[0]),
        pltpu.make_async_copy(sol_hbm, sol, load_sem.at[1]),
        pltpu.make_async_copy(rhs_hbm, rhs, load_sem.at[2]),
        pltpu.make_async_copy(dia_hbm.at[0], dia, load_sem.at[3]),
    ]
    for load in loads:
        load.start()

    barrier = pltpu.get_barrier_semaphore()
    for peer in (up, down):
        pl.semaphore_signal(barrier, inc=1, device_id=(col, peer), device_id_type=MESH)
    for hop in range(1, hops + 1):
        for peer in (lax.rem(col + hop, n_col), lax.rem(col + n_col - hop, n_col)):
            pl.semaphore_signal(barrier, inc=1, device_id=(peer, row), device_id_type=MESH)
    pl.semaphore_wait(barrier, 2 + 2 * hops)

    def y_copy(src, tile, start, size, kind, peer):
        return pltpu.make_async_remote_copy(
            src_ref=src,
            dst_ref=fac.at[tile, pl.ds(start, size), :],
            send_sem=y_send.at[tile, kind],
            recv_sem=y_recv.at[tile, kind],
            device_id=(col, peer),
            device_id_type=MESH,
        )

    def own(tile):
        return (
            y_copy(fac_hbm.at[0, tile], tile, quarter, quarter, 0, up),
            y_copy(fac_hbm.at[0, tile], tile, 2 * quarter, quarter, 1, down),
        )

    def relay(tile):
        return (
            y_copy(fac.at[tile, pl.ds(quarter, half), :], tile, 3 * quarter, half, 2, up),
            y_copy(fac.at[tile, pl.ds(2 * quarter + half, half), :], tile, 3 * quarter + half, half, 3, down),
        )

    def product(tile, start, size):
        weight = tiles_ref[0, tile].astype(jnp.float32)

        @pl.loop(0, cols // wide)
        def _(block):
            at = pl.ds(pl.multiple_of(block * wide, wide), wide)
            term = jnp.dot(
                fac[tile, pl.ds(start, size), :], sol[:, at], preferred_element_type=jnp.float32
            )
            part[tile, pl.ds(start, size), at] = (term * weight).astype(jnp.bfloat16)

    def send(tile, start, size, kind):
        return pltpu.make_async_remote_copy(
            src_ref=part.at[tile, pl.ds(start, size), :],
            dst_ref=got.at[tile, pl.ds(start, size), :],
            send_sem=x_send.at[kind],
            recv_sem=x_recv.at[kind],
            device_id=(lax.rem(col + tile + 1, n_col), row),
            device_id_type=MESH,
        )

    def add(tile, start, size, first=False):
        at = pl.ds(start, size)
        term = got[tile, at, :].astype(jnp.float32)
        acc[at, :] = term if first else acc[at, :] + term

    sends = []

    def go(copy):
        copy.start()
        sends.append(copy)

    for tile in order[:2]:
        for copy in own(tile):
            go(copy)
    loads[0].wait()
    loads[1].wait()

    arrivals = []
    for step, tile in enumerate(order):
        for copy, onward in zip(own(tile), relay(tile)):
            copy.wait_recv()
            go(onward)
        if step + 2 < hops:
            for copy in own(order[step + 2]):
                go(copy)
        if step >= 1:
            before = order[step - 1]
            for copy in relay(before):
                copy.wait_recv()
            product(before, 0, rows)
            out = send(before, 0, rows, before)
            go(out)
            arrivals.append((before, out))
        if step >= 3:
            done, arrival = arrivals.pop(0)
            arrival.wait_recv()
            add(done, 0, rows, first=step == 3)
    last = order[-1]
    product(last, 0, 3 * quarter)
    early = send(last, 0, 3 * quarter, last)
    go(early)
    for copy in relay(last):
        copy.wait_recv()
    product(last, 3 * quarter, quarter)
    late = send(last, 3 * quarter, quarter, hops)
    go(late)
    loads[2].wait()
    loads[3].wait()
    for done, arrival in arrivals:
        arrival.wait_recv()
        add(done, 0, rows)
    for arrival, start, size in ((early, 0, 3 * quarter), (late, 3 * quarter, quarter)):
        arrival.wait_recv()
        add(last, start, size)
    for slot, peer in enumerate((row, down, up, lax.rem(row + 2, n_rhs))):
        at = pl.ds(pl.multiple_of(peer * quarter, quarter), quarter)
        rem[at, :] = (
            rhs[at, :].astype(jnp.float32) - acc[pl.ds(slot * quarter, quarter), :]
        ).astype(jnp.bfloat16)
    out_ref[...] = jnp.dot(dia[...], rem[...], preferred_element_type=jnp.float32).astype(jnp.bfloat16)
    for copy in sends:
        copy.wait_send()


ORDER = (3, 4, 2, 5, 1, 0)


def per_device(rhs_block, sol, factor, tile_list, diag_inverse):
    n_col, n_rhs = lax.axis_size("col"), lax.axis_size("rhs")
    rows, cols = rhs_block.shape
    depth = sol.shape[0]
    hops = factor.shape[1]
    any_space = pl.BlockSpec(memory_space=pl.ANY)
    return pl.pallas_call(
        functools.partial(kernel, n_col, n_rhs, ORDER),
        out_shape=jax.ShapeDtypeStruct((rows, cols), jnp.bfloat16),
        in_specs=[pl.BlockSpec(memory_space=pltpu.SMEM)] + [any_space] * 4,
        out_specs=pl.BlockSpec(memory_space=pltpu.VMEM),
        scratch_shapes=[
            pltpu.VMEM((depth, cols), jnp.bfloat16),
            pltpu.VMEM((hops, rows, depth), jnp.bfloat16),
            pltpu.VMEM((rows, cols), jnp.bfloat16),
            pltpu.VMEM((rows, rows), jnp.bfloat16),
            pltpu.VMEM((rows, cols), jnp.float32),
            pltpu.VMEM((rows, cols), jnp.bfloat16),
            pltpu.VMEM((hops, rows, cols), jnp.bfloat16),
            pltpu.VMEM((hops, rows, cols), jnp.bfloat16),
            pltpu.SemaphoreType.DMA((4,)),
            pltpu.SemaphoreType.DMA((hops, 4)),
            pltpu.SemaphoreType.DMA((hops, 4)),
            pltpu.SemaphoreType.DMA((hops + 1,)),
            pltpu.SemaphoreType.DMA((hops + 1,)),
        ],
        compiler_params=pltpu.CompilerParams(
            collective_id=0, has_side_effects=True, vmem_limit_bytes=60 * 1024 * 1024
        ),
    )(tile_list, rhs_block, sol, factor, diag_inverse)


def solution(mesh):
    in_specs = (
        P("col", "rhs"),
        P("col", "rhs"),
        P("col", None, "rhs", None),
        P("col", None),
        P("col", None, None),
    )
    return jax.shard_map(
        per_device, mesh=mesh, in_specs=in_specs, out_specs=P("col", "rhs"), check_vma=False
    )
```

```python
import functools

import jax
import jax.numpy as jnp
from jax import lax
from jax.experimental import pallas as pl
from jax.experimental.pallas import tpu as pltpu
from jax.sharding import PartitionSpec as P

MESH = pl.DeviceIdType.MESH
PAIRED = (4, 5, 6, 3, 2)
PIECES = 4


def kernel(n_col, n_rhs, tiles_ref, rhs_hbm, sol_hbm, fac_hbm, dia_hbm, out_ref,
           sol, fac, rhs, dia, acc, rem, keep, give, take, part, got, tail, near, last,
           load_sem, y_send, y_recv, z_send, z_recv, c_send, c_recv, x_send, x_recv, t_send, t_recv, turn):
    hops, quarter = fac_hbm.shape[1], fac_hbm.shape[2]
    depth = fac_hbm.shape[3]
    rows, cols = rhs_hbm.shape
    half = quarter // 2
    side = cols // 2
    wide = min(256, side)
    piece = depth // PIECES
    most = rows - quarter
    pairs = len(PAIRED)
    col, row = lax.axis_index("col"), lax.axis_index("rhs")
    core = lax.rem(col, 2)
    base = col - core
    partner = base + 1 - core
    up, down = lax.rem(row + 1, n_rhs), lax.rem(row + n_rhs - 1, n_rhs)
    tile_of = [ahead - 1 - core for ahead in PAIRED] + [(hops - 1) * core]

    loads = [
        pltpu.make_async_copy(fac_hbm.at[0, tile_of[s]], fac.at[s, pl.ds(0, quarter), :], load_sem.at[s])
        for s in range(hops)
    ]
    loads += [
        pltpu.make_async_copy(sol_hbm, sol, load_sem.at[hops]),
        pltpu.make_async_copy(rhs_hbm, rhs, load_sem.at[hops + 1]),
        pltpu.make_async_copy(dia_hbm.at[0], dia, load_sem.at[hops + 2]),
    ]

    barrier = pltpu.get_barrier_semaphore()
    for peer in (up, down):
        pl.semaphore_signal(barrier, inc=1, device_id=(col, peer), device_id_type=MESH)
    pl.semaphore_signal(barrier, inc=1, device_id=(partner, row), device_id_type=MESH)
    for back in (2, 4, 6):
        for which in (0, 1):
            source = lax.rem(base + n_col - back + which, n_col)
            pl.semaphore_signal(barrier, inc=1, device_id=(source, row), device_id_type=MESH)
    for load in loads:
        load.start()
    pl.semaphore_wait(barrier, 9)

    def remote(src, dst, send, recv, device):
        return pltpu.make_async_remote_copy(
            src_ref=src, dst_ref=dst, send_sem=send, recv_sem=recv, device_id=device, device_id_type=MESH
        )

    def y_copy(src, s, start, size, kind, peer):
        return remote(
            src, fac.at[s, pl.ds(start, size), :], y_send.at[s, kind], y_recv.at[s, kind], (col, peer)
        )

    def own(s):
        src = fac_hbm.at[0, tile_of[s]]
        return (
            y_copy(src, s, quarter, quarter, 0, up),
            y_copy(src, s, 2 * quarter, quarter, 1, down),
        )

    def relay(s):
        return (
            y_copy(fac.at[s, pl.ds(quarter, half), :], s, 3 * quarter, half, 2, up),
            y_copy(fac.at[s, pl.ds(2 * quarter + half, half), :], s, 3 * quarter + half, half, 3, down),
        )

    final = hops - 1

    def z_copy(src, p, start, size, kind, peer):
        at = pl.ds(p * piece, piece)
        return remote(
            src.at[:, at], fac.at[final, pl.ds(start, size), at], z_send.at[p, kind], z_recv.at[p, kind], (col, peer)
        )

    def own_piece(p):
        src = fac_hbm.at[0, tile_of[final]]
        return (
            z_copy(src, p, quarter, quarter, 0, up),
            z_copy(src, p, 2 * quarter, quarter, 1, down),
        )

    def relay_piece(p):
        return (
            z_copy(fac.at[final, pl.ds(quarter, half), :], p, 3 * quarter, half, 2, up),
            z_copy(fac.at[final, pl.ds(2 * quarter + half, half), :], p, 3 * quarter + half, half, 3, down),
        )

    def weight(s):
        return tiles_ref[0, tile_of[s]].astype(jnp.float32)

    def product(s):
        scale = weight(s)
        for target, which in ((give, 1 - core), (keep, core)):

            @pl.loop(0, side // wide)
            def _(block):
                at = pl.multiple_of(which * side + block * wide, wide)
                term = jnp.dot(fac[s], sol[:, pl.ds(at, wide)], preferred_element_type=jnp.float32)
                target[s, :, pl.ds(pl.multiple_of(block * wide, wide), wide)] = term * scale

            if target is give:
                swap(s).start()

    def swap(s):
        return remote(give.at[s], take.at[s], c_send.at[s], c_recv.at[s], (partner, row))

    def onward(s):
        ahead = PAIRED[s]
        slot = ahead // 2 - 1
        return remote(
            part.at[s], got.at[slot, core], x_send.at[s], x_recv.at[slot, core],
            (lax.rem(base + ahead, n_col), row),
        )

    def combine(s):
        swap(s).wait_recv()
        part[s] = (keep[s] + take[s]).astype(jnp.bfloat16)
        onward(s).start()

    def arrived(slot, which):
        return remote(part.at[0], got.at[slot, which], x_send.at[0], x_recv.at[slot, which], (partner, row))

    def add(slot, first=False):
        for which in (0, 1):
            arrived(slot, which).wait_recv()
            at = pl.ds(which * side, side)
            term = got[slot, which].astype(jnp.float32)
            acc[:, at] = term if first else acc[:, at] + term

    def close(start, size, kind):
        at = pl.ds(start, size)
        inside = remote(tail.at[at, :], near.at[at, :], t_send.at[kind], t_recv.at[0, kind], (partner, row))
        outside = remote(
            last.at[:, at, :], got.at[2, :, at, :], t_send.at[kind], t_recv.at[1, kind],
            (lax.rem(base + 7, n_col), row),
        )
        return inside, outside

    def product_most():
        scale = weight(final)

        @pl.loop(0, cols // wide)
        def _(block):
            at = pl.ds(pl.multiple_of(block * wide, wide), wide)
            term = jnp.dot(
                fac[final, pl.ds(0, most), :], sol[:, at], preferred_element_type=jnp.float32
            )
            tail[pl.ds(0, most), at] = term * scale

    def hand_over(start, size, kind):
        inside, outside = close(start, size, kind)

        @pl.when(core == 0)
        def _():
            inside.start()

        @pl.when(core == 1)
        def _():
            at = pl.ds(start, size)
            for which in (0, 1):
                last[which, at, :] = tail[at, pl.ds(which * side, side)].astype(jnp.bfloat16)
            outside.start()

    for s in (0, 1):
        for copy in own(s):
            copy.start()
    for load in loads:
        load.wait()

    for s in range(pairs):
        for copy, forward in zip(own(s), relay(s)):
            copy.wait_recv()
            forward.start()
        if s + 2 < pairs:
            for copy in own(s + 2):
                copy.start()
        elif s + 2 == pairs:

            @pl.when(core == 1)
            def _():
                for p in range(PIECES):
                    for copy in own_piece(p):
                        copy.start()

        if s >= 1:
            for copy in relay(s - 1):
                copy.wait_recv()
            product(s - 1)
        if s >= 2:
            combine(s - 2)
        if s == 4:
            add(1, first=True)

    def pass_on():
        for p in range(PIECES):
            for copy, forward in zip(own_piece(p), relay_piece(p)):
                copy.wait_recv()
                forward.start()

    @pl.when(core == 1)
    def _():
        pass_on()
        pl.semaphore_signal(turn, inc=1, device_id=(partner, row), device_id_type=MESH)
        product_most()

    for copy in relay(pairs - 1):
        copy.wait_recv()
    product(pairs - 1)

    @pl.when(core == 0)
    def _():
        pl.semaphore_wait(turn, 1)
        for p in range(PIECES):
            for copy in own_piece(p):
                copy.start()

    combine(pairs - 2)
    combine(pairs - 1)

    @pl.when(core == 0)
    def _():
        pass_on()
        product_most()

    hand_over(0, most, 0)
    for p in range(PIECES):
        for copy in relay_piece(p):
            copy.wait_recv()
        deep = pl.ds(p * piece, piece)

        @pl.loop(0, cols // wide)
        def _(block):
            at = pl.ds(pl.multiple_of(block * wide, wide), wide)
            term = jnp.dot(
                fac[final, pl.ds(most, quarter), deep], sol[deep, at], preferred_element_type=jnp.float32
            )
            if p > 0:
                term = term + tail[pl.ds(most, quarter), at]
            if p == PIECES - 1:
                term = term * weight(final)
            tail[pl.ds(most, quarter), at] = term

    hand_over(most, quarter, 1)
    add(0)

    @pl.when(core == 0)
    def _():
        add(2)

    @pl.when(core == 1)
    def _():
        for kind, start, size in ((0, 0, most), (1, most, quarter)):
            at = pl.ds(start, size)
            inside, outside = close(start, size, kind)
            outside.wait_recv()
            for which in (0, 1):
                there = pl.ds(which * side, side)
                acc[at, there] = acc[at, there] + got[2, which, at, :].astype(jnp.float32)
            inside.wait_recv()
            acc[at, :] = acc[at, :] + near[at, :]

    for slot, peer in enumerate((row, down, up, lax.rem(row + 2, n_rhs))):
        at = pl.ds(pl.multiple_of(peer * quarter, quarter), quarter)
        rem[at, :] = (
            rhs[at, :].astype(jnp.float32) - acc[pl.ds(slot * quarter, quarter), :]
        ).astype(jnp.bfloat16)
    out_ref[...] = jnp.dot(dia[...], rem[...], preferred_element_type=jnp.float32).astype(jnp.bfloat16)

    for s in range(pairs):
        for copy in own(s) + relay(s) + (swap(s), onward(s)):
            copy.wait_send()
    for p in range(PIECES):
        for copy in own_piece(p) + relay_piece(p):
            copy.wait_send()
    for kind, start, size in ((0, 0, most), (1, most, quarter)):
        inside, outside = close(start, size, kind)

        @pl.when(core == 0)
        def _():
            inside.wait_send()

        @pl.when(core == 1)
        def _():
            outside.wait_send()


def per_device(rhs_block, sol, factor, tile_list, diag_inverse):
    n_col, n_rhs = lax.axis_size("col"), lax.axis_size("rhs")
    rows, cols = rhs_block.shape
    depth = sol.shape[0]
    hops = factor.shape[1]
    pairs, side = len(PAIRED), cols // 2
    any_space = pl.BlockSpec(memory_space=pl.ANY)
    dma = pltpu.SemaphoreType.DMA
    return pl.pallas_call(
        functools.partial(kernel, n_col, n_rhs),
        out_shape=jax.ShapeDtypeStruct((rows, cols), jnp.bfloat16),
        in_specs=[pl.BlockSpec(memory_space=pltpu.SMEM)] + [any_space] * 4,
        out_specs=pl.BlockSpec(memory_space=pltpu.VMEM),
        scratch_shapes=[
            pltpu.VMEM((depth, cols), jnp.bfloat16),
            pltpu.VMEM((hops, rows, depth), jnp.bfloat16),
            pltpu.VMEM((rows, cols), jnp.bfloat16),
            pltpu.VMEM((rows, rows), jnp.bfloat16),
            pltpu.VMEM((rows, cols), jnp.float32),
            pltpu.VMEM((rows, cols), jnp.bfloat16),
            pltpu.VMEM((pairs, rows, side), jnp.float32),
            pltpu.VMEM((pairs, rows, side), jnp.float32),
            pltpu.VMEM((pairs, rows, side), jnp.float32),
            pltpu.VMEM((pairs, rows, side), jnp.bfloat16),
            pltpu.VMEM((3, 2, rows, side), jnp.bfloat16),
            pltpu.VMEM((rows, cols), jnp.float32),
            pltpu.VMEM((rows, cols), jnp.float32),
            pltpu.VMEM((2, rows, side), jnp.bfloat16),
            dma((hops + 3,)),
            dma((pairs, 4)),
            dma((pairs, 4)),
            dma((PIECES, 4)),
            dma((PIECES, 4)),
            dma((pairs,)),
            dma((pairs,)),
            dma((pairs,)),
            dma((3, 2)),
            dma((2,)),
            dma((2, 2)),
            pltpu.SemaphoreType.REGULAR,
        ],
        compiler_params=pltpu.CompilerParams(
            collective_id=0, has_side_effects=True, vmem_limit_bytes=60 * 1024 * 1024
        ),
    )(tile_list, rhs_block, sol, factor, diag_inverse)


def solution(mesh):
    in_specs = (
        P("col", "rhs"),
        P("col", "rhs"),
        P("col", None, "rhs", None),
        P("col", None),
        P("col", None, None),
    )
    return jax.shard_map(
        per_device, mesh=mesh, in_specs=in_specs, out_specs=P("col", "rhs"), check_vma=False
    )
```

```python
import functools

import jax
import jax.numpy as jnp
from jax import lax
from jax.experimental import pallas as pl
from jax.experimental.pallas import tpu as pltpu
from jax.sharding import PartitionSpec as P

MESH = pl.DeviceIdType.MESH
PAIRED = (4, 5, 6, 3, 2)
PIECES = 4


def kernel(n_col, n_rhs, tiles_ref, rhs_hbm, sol_hbm, fac_hbm, dia_hbm, out_ref,
           sol, fac, rhs, dia, acc, rem, keep, give, take, part, got, tail, near, last,
           load_sem, y_send, y_recv, z_send, z_recv, c_send, c_recv, x_send, x_recv, t_send, t_recv, turn):
    hops, quarter = fac_hbm.shape[1], fac_hbm.shape[2]
    depth = fac_hbm.shape[3]
    rows, cols = rhs_hbm.shape
    half = quarter // 2
    side = cols // 2
    wide = min(256, side)
    piece = depth // PIECES
    most = rows - quarter
    pairs = len(PAIRED)
    col, row = lax.axis_index("col"), lax.axis_index("rhs")
    core = lax.rem(col, 2)
    base = col - core
    partner = base + 1 - core
    up, down = lax.rem(row + 1, n_rhs), lax.rem(row + n_rhs - 1, n_rhs)
    tile_of = [ahead - 1 - core for ahead in PAIRED] + [(hops - 1) * core]

    loads = [
        pltpu.make_async_copy(fac_hbm.at[0, tile_of[s]], fac.at[s, pl.ds(0, quarter), :], load_sem.at[s])
        for s in range(hops)
    ]
    loads += [
        pltpu.make_async_copy(sol_hbm, sol, load_sem.at[hops]),
        pltpu.make_async_copy(rhs_hbm, rhs, load_sem.at[hops + 1]),
        pltpu.make_async_copy(dia_hbm.at[0], dia, load_sem.at[hops + 2]),
    ]

    barrier = pltpu.get_barrier_semaphore()
    for peer in (up, down):
        pl.semaphore_signal(barrier, inc=1, device_id=(col, peer), device_id_type=MESH)
    pl.semaphore_signal(barrier, inc=1, device_id=(partner, row), device_id_type=MESH)
    for back in (2, 4, 6):
        for which in (0, 1):
            source = lax.rem(base + n_col - back + which, n_col)
            pl.semaphore_signal(barrier, inc=1, device_id=(source, row), device_id_type=MESH)
    for load in loads:
        load.start()
    pl.semaphore_wait(barrier, 9)

    def remote(src, dst, send, recv, device):
        return pltpu.make_async_remote_copy(
            src_ref=src, dst_ref=dst, send_sem=send, recv_sem=recv, device_id=device, device_id_type=MESH
        )

    def y_copy(src, s, start, size, kind, peer):
        return remote(
            src, fac.at[s, pl.ds(start, size), :], y_send.at[s, kind], y_recv.at[s, kind], (col, peer)
        )

    def own(s):
        src = fac_hbm.at[0, tile_of[s]]
        return (
            y_copy(src, s, quarter, quarter, 0, up),
            y_copy(src, s, 2 * quarter, quarter, 1, down),
        )

    def relay(s):
        return (
            y_copy(fac.at[s, pl.ds(quarter, half), :], s, 3 * quarter, half, 2, up),
            y_copy(fac.at[s, pl.ds(2 * quarter + half, half), :], s, 3 * quarter + half, half, 3, down),
        )

    final = hops - 1

    def z_copy(src, p, start, size, kind, peer):
        at = pl.ds(p * piece, piece)
        return remote(
            src.at[:, at], fac.at[final, pl.ds(start, size), at], z_send.at[p, kind], z_recv.at[p, kind], (col, peer)
        )

    def own_piece(p):
        src = fac_hbm.at[0, tile_of[final]]
        return (
            z_copy(src, p, quarter, quarter, 0, up),
            z_copy(src, p, 2 * quarter, quarter, 1, down),
        )

    def relay_piece(p):
        return (
            z_copy(fac.at[final, pl.ds(quarter, half), :], p, 3 * quarter, half, 2, up),
            z_copy(fac.at[final, pl.ds(2 * quarter + half, half), :], p, 3 * quarter + half, half, 3, down),
        )

    def weight(s):
        return tiles_ref[0, tile_of[s]].astype(jnp.float32)

    early, late = (0, most, 0), (most, quarter, 1)

    def product(s, span):
        scale = weight(s)
        lines = pl.ds(span[0], span[1])
        for target, which in ((give, 1 - core), (keep, core)):

            @pl.loop(0, side // wide)
            def _(block):
                at = pl.multiple_of(which * side + block * wide, wide)
                term = jnp.dot(fac[s, lines, :], sol[:, pl.ds(at, wide)], preferred_element_type=jnp.float32)
                target[s, lines, pl.ds(pl.multiple_of(block * wide, wide), wide)] = term * scale

            if target is give:
                swap(s, span).start()

    def swap(s, span):
        start, size, kind = span
        at = pl.ds(start, size)
        return remote(
            give.at[s, at, :], take.at[s, at, :], c_send.at[s, kind], c_recv.at[s, kind], (partner, row)
        )

    def onward(s, span):
        start, size, kind = span
        at = pl.ds(start, size)
        slot = PAIRED[s] // 2 - 1
        return remote(
            part.at[s, at, :], got.at[slot, core, at, :], x_send.at[s, kind], x_recv.at[slot, kind, core],
            (lax.rem(base + PAIRED[s], n_col), row),
        )

    def combine(s, span):
        at = pl.ds(span[0], span[1])
        swap(s, span).wait_recv()
        part[s, at, :] = (keep[s, at, :] + take[s, at, :]).astype(jnp.bfloat16)
        onward(s, span).start()

    def add(slot, span, first=False):
        start, size, kind = span
        at = pl.ds(start, size)
        for which in (0, 1):
            remote(
                part.at[0, at, :], got.at[slot, which, at, :], x_send.at[0, 0], x_recv.at[slot, kind, which],
                (partner, row),
            ).wait_recv()
            there = pl.ds(which * side, side)
            term = got[slot, which, at, :].astype(jnp.float32)
            acc[at, there] = term if first else acc[at, there] + term

    def close(start, size, kind):
        at = pl.ds(start, size)
        inside = remote(tail.at[at, :], near.at[at, :], t_send.at[kind], t_recv.at[0, kind], (partner, row))
        outside = remote(
            last.at[:, at, :], got.at[2, :, at, :], t_send.at[kind], t_recv.at[1, kind],
            (lax.rem(base + 7, n_col), row),
        )
        return inside, outside

    def partial(p, span):
        lines, deep = pl.ds(span[0], span[1]), pl.ds(p * piece, piece)

        @pl.loop(0, cols // wide)
        def _(block):
            at = pl.ds(pl.multiple_of(block * wide, wide), wide)
            term = jnp.dot(fac[final, lines, deep], sol[deep, at], preferred_element_type=jnp.float32)
            if p > 0:
                term = term + tail[lines, at]
            if p == PIECES - 1:
                term = term * weight(final)
            tail[lines, at] = term

    def hand_over(start, size, kind):
        inside, outside = close(start, size, kind)

        @pl.when(core == 0)
        def _():
            inside.start()

        @pl.when(core == 1)
        def _():
            at = pl.ds(start, size)
            for which in (0, 1):
                last[which, at, :] = tail[at, pl.ds(which * side, side)].astype(jnp.bfloat16)
            outside.start()

    for s in (0, 1):
        for copy in own(s):
            copy.start()
    for load in loads:
        load.wait()

    end = pairs - 1
    for s in range(pairs):
        for copy, forward in zip(own(s), relay(s)):
            copy.wait_recv()
            forward.start()
        if s + 2 < pairs:
            for copy in own(s + 2):
                copy.start()
        if s == end:

            @pl.when(core == 1)
            def _():
                for p in range(PIECES):
                    for copy in own_piece(p):
                        copy.start()

        product(s, early)
        combine(s, early)
        if s >= 1:
            for copy in relay(s - 1):
                copy.wait_recv()
            product(s - 1, late)
            combine(s - 1, late)
    for span in (early, late):
        add(1, span, first=True)
    for copy in relay(end):
        copy.wait_recv()
    product(end, late)
    combine(end, late)

    @pl.when(core == 0)
    def _():
        pl.semaphore_wait(turn, 1)
        for p in range(PIECES):
            for copy in own_piece(p):
                copy.start()
        for span in (early, late):
            add(2, span)

    for p in range(PIECES):
        if p == PIECES - 1:

            @pl.when(core == 1)
            def _():
                pl.semaphore_signal(turn, inc=1, device_id=(partner, row), device_id_type=MESH)

        for copy, forward in zip(own_piece(p), relay_piece(p)):
            copy.wait_recv()
            forward.start()
        partial(p, early)
    hand_over(*early)
    for p in range(PIECES):
        for copy in relay_piece(p):
            copy.wait_recv()
        partial(p, late)
    hand_over(*late)

    @pl.when(core == 0)
    def _():
        for span in (early, late):
            add(0, span)

    @pl.when(core == 1)
    def _():
        for span in (early, late):
            add(0, span)
        for start, size, kind in (early, late):
            at = pl.ds(start, size)
            inside, outside = close(start, size, kind)
            outside.wait_recv()
            for which in (0, 1):
                there = pl.ds(which * side, side)
                acc[at, there] = acc[at, there] + got[2, which, at, :].astype(jnp.float32)
            inside.wait_recv()
            acc[at, :] = acc[at, :] + near[at, :]

    for slot, peer in enumerate((row, down, up, lax.rem(row + 2, n_rhs))):
        at = pl.ds(pl.multiple_of(peer * quarter, quarter), quarter)
        rem[at, :] = (
            rhs[at, :].astype(jnp.float32) - acc[pl.ds(slot * quarter, quarter), :]
        ).astype(jnp.bfloat16)
    out_ref[...] = jnp.dot(dia[...], rem[...], preferred_element_type=jnp.float32).astype(jnp.bfloat16)

    for s in range(pairs):
        for copy in own(s) + relay(s) + tuple(f(s, span) for f in (swap, onward) for span in (early, late)):
            copy.wait_send()
    for p in range(PIECES):
        for copy in own_piece(p) + relay_piece(p):
            copy.wait_send()
    for start, size, kind in (early, late):
        inside, outside = close(start, size, kind)

        @pl.when(core == 0)
        def _():
            inside.wait_send()

        @pl.when(core == 1)
        def _():
            outside.wait_send()


def per_device(rhs_block, sol, factor, tile_list, diag_inverse):
    n_col, n_rhs = lax.axis_size("col"), lax.axis_size("rhs")
    rows, cols = rhs_block.shape
    depth = sol.shape[0]
    hops = factor.shape[1]
    pairs, side = len(PAIRED), cols // 2
    any_space = pl.BlockSpec(memory_space=pl.ANY)
    dma = pltpu.SemaphoreType.DMA
    return pl.pallas_call(
        functools.partial(kernel, n_col, n_rhs),
        out_shape=pltpu.VMEM((rows, cols), jnp.bfloat16),
        in_specs=[pl.BlockSpec(memory_space=pltpu.SMEM)] + [any_space] * 4,
        out_specs=pl.BlockSpec(memory_space=pltpu.VMEM),
        scratch_shapes=[
            pltpu.VMEM((depth, cols), jnp.bfloat16),
            pltpu.VMEM((hops, rows, depth), jnp.bfloat16),
            pltpu.VMEM((rows, cols), jnp.bfloat16),
            pltpu.VMEM((rows, rows), jnp.bfloat16),
            pltpu.VMEM((rows, cols), jnp.float32),
            pltpu.VMEM((rows, cols), jnp.bfloat16),
            pltpu.VMEM((pairs, rows, side), jnp.float32),
            pltpu.VMEM((pairs, rows, side), jnp.float32),
            pltpu.VMEM((pairs, rows, side), jnp.float32),
            pltpu.VMEM((pairs, rows, side), jnp.bfloat16),
            pltpu.VMEM((3, 2, rows, side), jnp.bfloat16),
            pltpu.VMEM((rows, cols), jnp.float32),
            pltpu.VMEM((rows, cols), jnp.float32),
            pltpu.VMEM((2, rows, side), jnp.bfloat16),
            dma((hops + 3,)),
            dma((pairs, 4)),
            dma((pairs, 4)),
            dma((PIECES, 4)),
            dma((PIECES, 4)),
            dma((pairs, 2)),
            dma((pairs, 2)),
            dma((pairs, 2)),
            dma((3, 2, 2)),
            dma((2,)),
            dma((2, 2)),
            pltpu.SemaphoreType.REGULAR,
        ],
        compiler_params=pltpu.CompilerParams(
            collective_id=0, has_side_effects=True, vmem_limit_bytes=60 * 1024 * 1024
        ),
    )(tile_list, rhs_block, sol, factor, diag_inverse)


def solution(mesh):
    in_specs = (
        P("col", "rhs"),
        P("col", "rhs"),
        P("col", None, "rhs", None),
        P("col", None),
        P("col", None, None),
    )
    return jax.shard_map(
        per_device, mesh=mesh, in_specs=in_specs, out_specs=P("col", "rhs"), check_vma=False
    )
```

```python
import functools

import jax
import jax.numpy as jnp
from jax import lax
from jax.experimental import pallas as pl
from jax.experimental.pallas import tpu as pltpu
from jax.sharding import PartitionSpec as P

MESH = pl.DeviceIdType.MESH
PAIRED = (4, 5, 6, 3, 2)
PIECES = 4


def kernel(n_col, n_rhs, tiles_ref, rhs_hbm, sol_hbm, fac_hbm, dia_hbm, out_ref,
           sol, fac, rhs, dia, acc, rem, keep, give, take, part, got, tail, near, last,
           load_sem, y_send, y_recv, z_send, z_recv, c_send, c_recv, x_send, x_recv, t_send, t_recv, turn):
    hops, quarter = fac_hbm.shape[1], fac_hbm.shape[2]
    depth = fac_hbm.shape[3]
    rows, cols = rhs_hbm.shape
    half = quarter // 2
    side = cols // 2
    wide = min(256, side)
    piece = depth // PIECES
    most = rows - quarter
    pairs = len(PAIRED)
    col, row = lax.axis_index("col"), lax.axis_index("rhs")
    core = lax.rem(col, 2)
    base = col - core
    partner = base + 1 - core
    up, down = lax.rem(row + 1, n_rhs), lax.rem(row + n_rhs - 1, n_rhs)
    tile_of = [ahead - 1 - core for ahead in PAIRED] + [(hops - 1) * core]

    loads = [
        pltpu.make_async_copy(fac_hbm.at[0, tile_of[s]], fac.at[s, pl.ds(0, quarter), :], load_sem.at[s])
        for s in range(hops)
    ]
    loads += [
        pltpu.make_async_copy(sol_hbm, sol, load_sem.at[hops]),
        pltpu.make_async_copy(rhs_hbm, rhs, load_sem.at[hops + 1]),
        pltpu.make_async_copy(dia_hbm.at[0], dia, load_sem.at[hops + 2]),
    ]

    barrier = pltpu.get_barrier_semaphore()
    for peer in (up, down):
        pl.semaphore_signal(barrier, inc=1, device_id=(col, peer), device_id_type=MESH)
    pl.semaphore_signal(barrier, inc=1, device_id=(partner, row), device_id_type=MESH)
    for back in (2, 4, 6):
        for which in (0, 1):
            source = lax.rem(base + n_col - back + which, n_col)
            pl.semaphore_signal(barrier, inc=1, device_id=(source, row), device_id_type=MESH)
    for load in loads:
        load.start()
    pl.semaphore_wait(barrier, 9)

    def remote(src, dst, send, recv, device):
        return pltpu.make_async_remote_copy(
            src_ref=src, dst_ref=dst, send_sem=send, recv_sem=recv, device_id=device, device_id_type=MESH
        )

    def y_copy(src, s, start, size, kind, peer):
        return remote(
            src, fac.at[s, pl.ds(start, size), :], y_send.at[s, kind], y_recv.at[s, kind], (col, peer)
        )

    def own(s):
        src = fac_hbm.at[0, tile_of[s]]
        return (
            y_copy(src, s, quarter, quarter, 0, up),
            y_copy(src, s, 2 * quarter, quarter, 1, down),
        )

    def relay(s):
        return (
            y_copy(fac.at[s, pl.ds(quarter, half), :], s, 3 * quarter, half, 2, up),
            y_copy(fac.at[s, pl.ds(2 * quarter + half, half), :], s, 3 * quarter + half, half, 3, down),
        )

    final = hops - 1

    def z_copy(src, p, start, size, kind, peer):
        at = pl.ds(p * piece, piece)
        return remote(
            src.at[:, at], fac.at[final, pl.ds(start, size), at], z_send.at[p, kind], z_recv.at[p, kind], (col, peer)
        )

    def own_piece(p):
        src = fac_hbm.at[0, tile_of[final]]
        return (
            z_copy(src, p, quarter, quarter, 0, up),
            z_copy(src, p, 2 * quarter, quarter, 1, down),
        )

    def relay_piece(p):
        return (
            z_copy(fac.at[final, pl.ds(quarter, half), :], p, 3 * quarter, half, 2, up),
            z_copy(fac.at[final, pl.ds(2 * quarter + half, half), :], p, 3 * quarter + half, half, 3, down),
        )

    def weight(s):
        return tiles_ref[0, tile_of[s]].astype(jnp.float32)

    early, late = (0, most, 0), (most, quarter, 1)

    def product(s, span):
        scale = weight(s)
        lines = pl.ds(span[0], span[1])
        for target, which in ((give, 1 - core), (keep, core)):

            @pl.loop(0, side // wide, unroll=True)
            def _(block):
                at = pl.multiple_of(which * side + block * wide, wide)
                term = jnp.dot(fac[s, lines, :], sol[:, pl.ds(at, wide)], preferred_element_type=jnp.float32)
                target[s, lines, pl.ds(pl.multiple_of(block * wide, wide), wide)] = term * scale

            if target is give:
                swap(s, span).start()

    def swap(s, span):
        start, size, kind = span
        at = pl.ds(start, size)
        return remote(
            give.at[s, at, :], take.at[s, at, :], c_send.at[s, kind], c_recv.at[s, kind], (partner, row)
        )

    def onward(s, span):
        start, size, kind = span
        at = pl.ds(start, size)
        slot = PAIRED[s] // 2 - 1
        return remote(
            part.at[s, at, :], got.at[slot, core, at, :], x_send.at[s, kind], x_recv.at[slot, kind, core],
            (lax.rem(base + PAIRED[s], n_col), row),
        )

    def combine(s, span):
        at = pl.ds(span[0], span[1])
        swap(s, span).wait_recv()
        part[s, at, :] = (keep[s, at, :] + take[s, at, :]).astype(jnp.bfloat16)
        onward(s, span).start()

    def add(slot, span, first=False):
        start, size, kind = span
        at = pl.ds(start, size)
        for which in (0, 1):
            remote(
                part.at[0, at, :], got.at[slot, which, at, :], x_send.at[0, 0], x_recv.at[slot, kind, which],
                (partner, row),
            ).wait_recv()
            there = pl.ds(which * side, side)
            term = got[slot, which, at, :].astype(jnp.float32)
            acc[at, there] = term if first else acc[at, there] + term

    def close(start, size, kind):
        at = pl.ds(start, size)
        inside = remote(tail.at[at, :], near.at[at, :], t_send.at[kind], t_recv.at[0, kind], (partner, row))
        outside = remote(
            last.at[:, at, :], got.at[2, :, at, :], t_send.at[kind], t_recv.at[1, kind],
            (lax.rem(base + 7, n_col), row),
        )
        return inside, outside

    def partial(p, span):
        lines, deep = pl.ds(span[0], span[1]), pl.ds(p * piece, piece)
        for block in range(2):
            at = pl.ds(block * side, side)
            term = jnp.dot(fac[final, lines, deep], sol[deep, at], preferred_element_type=jnp.float32)
            if p > 0:
                term = term + tail[lines, at]
            if p == PIECES - 1:
                term = term * weight(final)
            tail[lines, at] = term

    def hand_over(start, size, kind):
        inside, outside = close(start, size, kind)

        @pl.when(core == 0)
        def _():
            inside.start()

        @pl.when(core == 1)
        def _():
            at = pl.ds(start, size)
            for which in (0, 1):
                last[which, at, :] = tail[at, pl.ds(which * side, side)].astype(jnp.bfloat16)
            outside.start()

    for s in (0, 1):
        for copy in own(s):
            copy.start()
    for load in loads:
        load.wait()

    end = pairs - 1
    for s in range(pairs):
        for copy, forward in zip(own(s), relay(s)):
            copy.wait_recv()
            forward.start()
        if s + 2 < pairs:
            for copy in own(s + 2):
                copy.start()
        if s == end:

            @pl.when(core == 1)
            def _():
                for p in range(PIECES):
                    for copy in own_piece(p):
                        copy.start()

        product(s, early)
        if s >= 1:
            for copy in relay(s - 1):
                copy.wait_recv()
            product(s - 1, late)
        combine(s, early)
        if s >= 1:
            combine(s - 1, late)
    for span in (early, late):
        add(1, span, first=True)
    for copy in relay(end):
        copy.wait_recv()
    product(end, late)

    @pl.when(core == 0)
    def _():
        pl.semaphore_wait(turn, 1)
        for p in range(PIECES):
            for copy in own_piece(p):
                copy.start()
        combine(end, late)
        for span in (early, late):
            add(2, span)
        add(0, early)

    @pl.when(core == 1)
    def _():
        pl.semaphore_signal(turn, inc=1, device_id=(partner, row), device_id_type=MESH)

    for p in range(PIECES):
        for copy, forward in zip(own_piece(p), relay_piece(p)):
            copy.wait_recv()
            forward.start()
        if p == 1:

            @pl.when(core == 1)
            def _():
                combine(end, late)

        partial(p, early)
    hand_over(*early)
    for p in range(PIECES):
        for copy in relay_piece(p):
            copy.wait_recv()
        partial(p, late)
    hand_over(*late)

    def finish(span):
        start, size, kind = span
        at = pl.ds(start, size)
        inside, outside = close(start, size, kind)
        outside.wait_recv()
        for which in (0, 1):
            there = pl.ds(which * side, side)
            acc[at, there] = acc[at, there] + got[2, which, at, :].astype(jnp.float32)
        inside.wait_recv()
        acc[at, :] = acc[at, :] + near[at, :]

    def subtract(slot, peer):
        at = pl.ds(pl.multiple_of(peer * quarter, quarter), quarter)
        rem[at, :] = (
            rhs[at, :].astype(jnp.float32) - acc[pl.ds(slot * quarter, quarter), :]
        ).astype(jnp.bfloat16)

    @pl.when(core == 1)
    def _():
        for span in (early, late):
            add(0, span)
        finish(early)

    for slot, peer in enumerate((row, down, up)):
        subtract(slot, peer)

    @pl.when(core == 0)
    def _():
        add(0, late)

    @pl.when(core == 1)
    def _():
        finish(late)

    subtract(3, lax.rem(row + 2, n_rhs))
    out_ref[...] = jnp.dot(dia[...], rem[...], preferred_element_type=jnp.float32).astype(jnp.bfloat16)

    for s in range(pairs):
        for copy in own(s) + relay(s) + tuple(f(s, span) for f in (swap, onward) for span in (early, late)):
            copy.wait_send()
    for p in range(PIECES):
        for copy in own_piece(p) + relay_piece(p):
            copy.wait_send()
    for start, size, kind in (early, late):
        inside, outside = close(start, size, kind)

        @pl.when(core == 0)
        def _():
            inside.wait_send()

        @pl.when(core == 1)
        def _():
            outside.wait_send()


def per_device(rhs_block, sol, factor, tile_list, diag_inverse):
    n_col, n_rhs = lax.axis_size("col"), lax.axis_size("rhs")
    rows, cols = rhs_block.shape
    depth = sol.shape[0]
    hops = factor.shape[1]
    pairs, side = len(PAIRED), cols // 2
    any_space = pl.BlockSpec(memory_space=pl.ANY)
    dma = pltpu.SemaphoreType.DMA
    return pl.pallas_call(
        functools.partial(kernel, n_col, n_rhs),
        out_shape=pltpu.VMEM((rows, cols), jnp.bfloat16),
        in_specs=[pl.BlockSpec(memory_space=pltpu.SMEM)] + [any_space] * 4,
        out_specs=pl.BlockSpec(memory_space=pltpu.VMEM),
        scratch_shapes=[
            pltpu.VMEM((depth, cols), jnp.bfloat16),
            pltpu.VMEM((hops, rows, depth), jnp.bfloat16),
            pltpu.VMEM((rows, cols), jnp.bfloat16),
            pltpu.VMEM((rows, rows), jnp.bfloat16),
            pltpu.VMEM((rows, cols), jnp.float32),
            pltpu.VMEM((rows, cols), jnp.bfloat16),
            pltpu.VMEM((pairs, rows, side), jnp.float32),
            pltpu.VMEM((pairs, rows, side), jnp.float32),
            pltpu.VMEM((pairs, rows, side), jnp.float32),
            pltpu.VMEM((pairs, rows, side), jnp.bfloat16),
            pltpu.VMEM((3, 2, rows, side), jnp.bfloat16),
            pltpu.VMEM((rows, cols), jnp.float32),
            pltpu.VMEM((rows, cols), jnp.float32),
            pltpu.VMEM((2, rows, side), jnp.bfloat16),
            dma((hops + 3,)),
            dma((pairs, 4)),
            dma((pairs, 4)),
            dma((PIECES, 4)),
            dma((PIECES, 4)),
            dma((pairs, 2)),
            dma((pairs, 2)),
            dma((pairs, 2)),
            dma((3, 2, 2)),
            dma((2,)),
            dma((2, 2)),
            pltpu.SemaphoreType.REGULAR,
        ],
        compiler_params=pltpu.CompilerParams(
            collective_id=0, has_side_effects=True, vmem_limit_bytes=60 * 1024 * 1024
        ),
    )(tile_list, rhs_block, sol, factor, diag_inverse)


def solution(mesh):
    in_specs = (
        P("col", "rhs"),
        P("col", "rhs"),
        P("col", None, "rhs", None),
        P("col", None),
        P("col", None, None),
    )
    return jax.shard_map(
        per_device, mesh=mesh, in_specs=in_specs, out_specs=P("col", "rhs"), check_vma=False
    )
```

```python
import functools

import jax
import jax.numpy as jnp
from jax import lax
from jax.experimental import pallas as pl
from jax.experimental.pallas import tpu as pltpu
from jax.sharding import PartitionSpec as P

MESH = pl.DeviceIdType.MESH
PAIRED = (4, 5, 6, 3, 2)
PIECES = 4


def kernel(n_col, n_rhs, tiles_hbm, rhs_hbm, sol_hbm, fac_hbm, dia_hbm, out_ref,
           tiles_ref, sol, fac, rhs, dia, acc, rem, keep, give, take, part, got, tail, near, last,
           load_sem, y_send, y_recv, z_send, z_recv, c_send, c_recv, x_send, x_recv, t_send, t_recv, turn):
    hops, quarter = fac_hbm.shape[1], fac_hbm.shape[2]
    depth = fac_hbm.shape[3]
    rows, cols = rhs_hbm.shape
    half = quarter // 2
    side = cols // 2
    wide = min(256, side)
    piece = depth // PIECES
    most = rows - quarter
    pairs = len(PAIRED)
    col, row = lax.axis_index("col"), lax.axis_index("rhs")
    core = lax.rem(col, 2)
    base = col - core
    partner = base + 1 - core
    up, down = lax.rem(row + 1, n_rhs), lax.rem(row + n_rhs - 1, n_rhs)
    tile_of = [ahead - 1 - core for ahead in PAIRED] + [(hops - 1) * core]

    loads = [
        pltpu.make_async_copy(fac_hbm.at[0, tile_of[s]], fac.at[s, pl.ds(0, quarter), :], load_sem.at[s])
        for s in range(hops)
    ]
    loads += [
        pltpu.make_async_copy(sol_hbm, sol, load_sem.at[hops]),
        pltpu.make_async_copy(rhs_hbm, rhs, load_sem.at[hops + 1]),
        pltpu.make_async_copy(dia_hbm.at[0], dia, load_sem.at[hops + 2]),
        pltpu.make_async_copy(tiles_hbm, tiles_ref, load_sem.at[hops + 3]),
    ]

    barrier = pltpu.get_barrier_semaphore()
    for peer in (up, down):
        pl.semaphore_signal(barrier, inc=1, device_id=(col, peer), device_id_type=MESH)
    pl.semaphore_signal(barrier, inc=1, device_id=(partner, row), device_id_type=MESH)
    for back in (2, 4, 6):
        for which in (0, 1):
            source = lax.rem(base + n_col - back + which, n_col)
            pl.semaphore_signal(barrier, inc=1, device_id=(source, row), device_id_type=MESH)
    for load in loads:
        load.start()
    pl.semaphore_wait(barrier, 9)

    def remote(src, dst, send, recv, device):
        return pltpu.make_async_remote_copy(
            src_ref=src, dst_ref=dst, send_sem=send, recv_sem=recv, device_id=device, device_id_type=MESH
        )

    def y_copy(src, s, start, size, kind, peer):
        return remote(
            src, fac.at[s, pl.ds(start, size), :], y_send.at[s, kind], y_recv.at[s, kind], (col, peer)
        )

    def own(s):
        src = fac_hbm.at[0, tile_of[s]] if s < 2 else fac.at[s, pl.ds(0, quarter), :]
        return (
            y_copy(src, s, quarter, quarter, 0, up),
            y_copy(src, s, 2 * quarter, quarter, 1, down),
        )

    def relay(s):
        return (
            y_copy(fac.at[s, pl.ds(quarter, half), :], s, 3 * quarter, half, 2, up),
            y_copy(fac.at[s, pl.ds(2 * quarter + half, half), :], s, 3 * quarter + half, half, 3, down),
        )

    final = hops - 1

    def z_copy(src, p, start, size, kind, peer):
        at = pl.ds(p * piece, piece)
        return remote(
            src.at[:, at], fac.at[final, pl.ds(start, size), at], z_send.at[p, kind], z_recv.at[p, kind], (col, peer)
        )

    def own_piece(p):
        src = fac.at[final, pl.ds(0, quarter), :]
        return (
            z_copy(src, p, quarter, quarter, 0, up),
            z_copy(src, p, 2 * quarter, quarter, 1, down),
        )

    def relay_piece(p):
        return (
            z_copy(fac.at[final, pl.ds(quarter, half), :], p, 3 * quarter, half, 2, up),
            z_copy(fac.at[final, pl.ds(2 * quarter + half, half), :], p, 3 * quarter + half, half, 3, down),
        )

    def weight(s):
        return tiles_ref[0, tile_of[s]].astype(jnp.float32)

    early, late = (0, most, 0), (most, quarter, 1)

    def product(s, span):
        scale = weight(s)
        lines = pl.ds(span[0], span[1])
        for target, which in ((give, 1 - core), (keep, core)):

            @pl.loop(0, side // wide, unroll=True)
            def _(block):
                at = pl.multiple_of(which * side + block * wide, wide)
                term = jnp.dot(fac[s, lines, :], sol[:, pl.ds(at, wide)], preferred_element_type=jnp.float32)
                target[s, lines, pl.ds(pl.multiple_of(block * wide, wide), wide)] = term * scale

            if target is give:
                swap(s, span).start()

    def swap(s, span):
        start, size, kind = span
        at = pl.ds(start, size)
        return remote(
            give.at[s, at, :], take.at[s, at, :], c_send.at[s, kind], c_recv.at[s, kind], (partner, row)
        )

    def onward(s, span):
        start, size, kind = span
        at = pl.ds(start, size)
        slot = PAIRED[s] // 2 - 1
        return remote(
            part.at[s, at, :], got.at[slot, core, at, :], x_send.at[s, kind], x_recv.at[slot, kind, core],
            (lax.rem(base + PAIRED[s], n_col), row),
        )

    def combine(s, span):
        at = pl.ds(span[0], span[1])
        swap(s, span).wait_recv()
        part[s, at, :] = (keep[s, at, :] + take[s, at, :]).astype(jnp.bfloat16)
        onward(s, span).start()

    def add(slot, span, first=False):
        start, size, kind = span
        at = pl.ds(start, size)
        for which in (0, 1):
            remote(
                part.at[0, at, :], got.at[slot, which, at, :], x_send.at[0, 0], x_recv.at[slot, kind, which],
                (partner, row),
            ).wait_recv()
            there = pl.ds(which * side, side)
            term = got[slot, which, at, :].astype(jnp.float32)
            acc[at, there] = term if first else acc[at, there] + term

    def close(part_of):
        start, size, kind = early if part_of == 0 else late
        at, sides = pl.ds(start, size), (0, 1) if part_of == 0 else (part_of - 1,)
        there = pl.ds(sides[0] * side, len(sides) * side)
        which = pl.ds(sides[0], len(sides))
        inside = remote(
            tail.at[at, there], near.at[at, there], t_send.at[part_of], t_recv.at[0, part_of], (partner, row)
        )
        outside = remote(
            last.at[which, at, :], got.at[2, which, at, :], t_send.at[part_of], t_recv.at[1, part_of],
            (lax.rem(base + 7, n_col), row),
        )
        return inside, outside, at, sides

    def partial(p, span, blocks=(0, 1)):
        lines, deep = pl.ds(span[0], span[1]), pl.ds(p * piece, piece)
        for block in blocks:
            at = pl.ds(block * side, side)
            term = jnp.dot(fac[final, lines, deep], sol[deep, at], preferred_element_type=jnp.float32)
            if p > 0:
                term = term + tail[lines, at]
            if p == PIECES - 1:
                term = term * weight(final)
            tail[lines, at] = term

    def hand_over(part_of):
        inside, outside, at, sides = close(part_of)

        @pl.when(core == 0)
        def _():
            inside.start()

        @pl.when(core == 1)
        def _():
            for which in sides:
                last[which, at, :] = tail[at, pl.ds(which * side, side)].astype(jnp.bfloat16)
            outside.start()

    for s in (0, 1):
        for copy in own(s):
            copy.start()
    for load in loads:
        load.wait()

    end = pairs - 1
    for s in range(pairs):
        for copy, forward in zip(own(s), relay(s)):
            copy.wait_recv()
            forward.start()
        if s + 2 < pairs:
            for copy in own(s + 2):
                copy.start()
        if s == end:

            @pl.when(core == 1)
            def _():
                for p in range(PIECES):
                    for copy in own_piece(p):
                        copy.start()

        product(s, early)
        if s >= 1:
            for copy in relay(s - 1):
                copy.wait_recv()
            product(s - 1, late)
        combine(s, early)
        if s >= 1:
            combine(s - 1, late)
    for span in (early, late):
        add(1, span, first=True)
    for copy in relay(end):
        copy.wait_recv()
    product(end, late)

    @pl.when(core == 0)
    def _():
        pl.semaphore_wait(turn, 1)
        for p in range(PIECES):
            for copy in own_piece(p):
                copy.start()
        combine(end, late)
        for span in (early, late):
            add(2, span)
        add(0, early)

    @pl.when(core == 1)
    def _():
        pl.semaphore_signal(turn, inc=1, device_id=(partner, row), device_id_type=MESH)

    for p in range(PIECES):
        for copy, forward in zip(own_piece(p), relay_piece(p)):
            copy.wait_recv()
            forward.start()
        if p == 1:

            @pl.when(core == 1)
            def _():
                combine(end, late)

        partial(p, early)
    hand_over(0)
    for p in range(PIECES):
        for copy in relay_piece(p):
            copy.wait_recv()
        if p < PIECES - 1:
            partial(p, late)
    for which in (0, 1):
        partial(PIECES - 1, late, (which,))
        hand_over(which + 1)

    def finish(part_of):
        inside, outside, at, sides = close(part_of)
        outside.wait_recv()
        for which in sides:
            there = pl.ds(which * side, side)
            acc[at, there] = acc[at, there] + got[2, which, at, :].astype(jnp.float32)
        inside.wait_recv()
        for which in sides:
            there = pl.ds(which * side, side)
            acc[at, there] = acc[at, there] + near[at, there]

    def subtract(slot, peer, there):
        at = pl.ds(pl.multiple_of(peer * quarter, quarter), quarter)
        rem[at, there] = (
            rhs[at, there].astype(jnp.float32) - acc[pl.ds(slot * quarter, quarter), there]
        ).astype(jnp.bfloat16)

    @pl.when(core == 1)
    def _():
        for span in (early, late):
            add(0, span)
        finish(0)

    for slot, peer in enumerate((row, down, up)):
        subtract(slot, peer, pl.ds(0, cols))

    @pl.when(core == 0)
    def _():
        add(0, late)

    for which in (0, 1):
        there = pl.ds(which * side, side)

        @pl.when(core == 1)
        def _():
            finish(which + 1)

        subtract(3, lax.rem(row + 2, n_rhs), there)
        out_ref[:, there] = jnp.dot(
            dia[...], rem[:, there], preferred_element_type=jnp.float32
        ).astype(jnp.bfloat16)

    for s in range(pairs):
        for copy in own(s) + relay(s) + tuple(f(s, span) for f in (swap, onward) for span in (early, late)):
            copy.wait_send()
    for p in range(PIECES):
        for copy in own_piece(p) + relay_piece(p):
            copy.wait_send()
    for part_of in range(3):
        inside, outside, _, _ = close(part_of)

        @pl.when(core == 0)
        def _():
            inside.wait_send()

        @pl.when(core == 1)
        def _():
            outside.wait_send()


def per_device(rhs_block, sol, factor, tile_list, diag_inverse):
    n_col, n_rhs = lax.axis_size("col"), lax.axis_size("rhs")
    rows, cols = rhs_block.shape
    depth = sol.shape[0]
    hops = factor.shape[1]
    pairs, side = len(PAIRED), cols // 2
    any_space = pl.BlockSpec(memory_space=pl.ANY)
    dma = pltpu.SemaphoreType.DMA
    return pl.pallas_call(
        functools.partial(kernel, n_col, n_rhs),
        out_shape=pltpu.VMEM((rows, cols), jnp.bfloat16),
        in_specs=[any_space] * 5,
        out_specs=pl.BlockSpec(memory_space=pltpu.VMEM),
        scratch_shapes=[
            pltpu.SMEM((1, hops), jnp.int32),
            pltpu.VMEM((depth, cols), jnp.bfloat16),
            pltpu.VMEM((hops, rows, depth), jnp.bfloat16),
            pltpu.VMEM((rows, cols), jnp.bfloat16),
            pltpu.VMEM((rows, rows), jnp.bfloat16),
            pltpu.VMEM((rows, cols), jnp.float32),
            pltpu.VMEM((rows, cols), jnp.bfloat16),
            pltpu.VMEM((pairs, rows, side), jnp.float32),
            pltpu.VMEM((pairs, rows, side), jnp.float32),
            pltpu.VMEM((pairs, rows, side), jnp.float32),
            pltpu.VMEM((pairs, rows, side), jnp.bfloat16),
            pltpu.VMEM((3, 2, rows, side), jnp.bfloat16),
            pltpu.VMEM((rows, cols), jnp.float32),
            pltpu.VMEM((rows, cols), jnp.float32),
            pltpu.VMEM((2, rows, side), jnp.bfloat16),
            dma((hops + 4,)),
            dma((pairs, 4)),
            dma((pairs, 4)),
            dma((PIECES, 4)),
            dma((PIECES, 4)),
            dma((pairs, 2)),
            dma((pairs, 2)),
            dma((pairs, 2)),
            dma((3, 2, 2)),
            dma((3,)),
            dma((2, 3)),
            pltpu.SemaphoreType.REGULAR,
        ],
        compiler_params=pltpu.CompilerParams(
            collective_id=0, has_side_effects=True, vmem_limit_bytes=60 * 1024 * 1024
        ),
    )(tile_list, rhs_block, sol, factor, diag_inverse)


def solution(mesh):
    in_specs = (
        P("col", "rhs"),
        P("col", "rhs"),
        P("col", None, "rhs", None),
        P("col", None),
        P("col", None, None),
    )
    return jax.shard_map(
        per_device, mesh=mesh, in_specs=in_specs, out_specs=P("col", "rhs"), check_vma=False
    )
```
